32 devices in a mesh: groups: 2 (over y), owner: 4 (over z), head: 2 (over x), rep: 2 (over core).
Axes of the slice: x: 2, y: 2, z: 4, core: 2. Of those that a mesh axis runs over, the one named last changes fastest.
Arguments:
- queries: bfloat16 [4096, 8, 512], P(('groups', 'owner', 'rep'), 'head'), parts along dimension 0, may hold values from -10 to 10
- cotangent: bfloat16 [4096, 8, 512], P(('groups', 'owner', 'rep'), 'head'), parts along dimension 0, may hold values from -6 to 6
- own_kv: bfloat16 [4096, 8, 256], P(('groups', 'owner', 'rep'), 'head'), parts along dimension 0, may hold values from -6 to 6
- tables: int32 [4096, 1], P(('groups', 'owner', 'rep')), parts along dimension 0, may hold values from 0 to 3; in each aligned block of 256 rows (0 to 255, 256 to 511, ...) at most 128 rows name the same one
- table_owner: int32 [8], P('groups'), parts along dimension 0, may hold values from 0 to 3, each once
- cache_keys: float32 [8, 8, 1024, 128], P(('groups', 'owner'), 'head', 'rep'), parts along dimension 0, may hold values from -10 to 10
- cache_values: float32 [8, 8, 1024, 128], P(('groups', 'owner'), 'head', 'rep'), parts along dimension 0, may hold values from -6 to 6
- first_moment: float32 [2, 8, 8, 1024, 128], P(None, ('groups', 'owner'), 'head', 'rep'), parts along dimension 1, may hold values from -0.75 to 0.75
- second_moment: float32 [2, 8, 8, 1024, 128], P(None, ('groups', 'owner'), 'head', 'rep'), parts along dimension 1, may hold values from 1e-06 to 0.1
Outputs:
- attended: bfloat16 [4096, 8, 512], P(('groups', 'owner', 'rep'), 'head'), parts along dimension 0
- new_keys: float32 [8, 8, 1024, 128], P(('groups', 'owner'), 'head', 'rep'), parts along dimension 0
- new_values: float32 [8, 8, 1024, 128], P(('groups', 'owner'), 'head', 'rep'), parts along dimension 0
- new_first: float32 [2, 8, 8, 1024, 128], P(None, ('groups', 'owner'), 'head', 'rep'), parts along dimension 1
- new_second: float32 [2, 8, 8, 1024, 128], P(None, ('groups', 'owner'), 'head', 'rep'), parts along dimension 1
The draws below stay inside these ranges and needn't reach their ends.
There are 2 independent parts, one for each index of `groups`. The reference program is written for one: setup_inputs(seed, part) draws one part's arguments, and reference() takes and returns one part's arrays. A program takes and returns all parts, laid end to end along the dimension named above; each array names one. Nothing has to cross between parts.
Inputs may be any that keep to these rules, and one draw needn't show every extreme that they name: `tables`: in the rows of one reader device no table is named by more than 128 tokens, a bound that some block reaches. `table_owner`: each owner holds exactly one table.
All inputs are finite; a program needn't handle non-finite values.
Results may differ from the reference program's by a relative error of at most 0.0085.
Values may be sent and summed in bfloat16 or wider, within the bound.
A program may use at most 128 MiB of HBM per device.

```python
import math
import jax
import jax.numpy as jnp
import numpy as np
from jax import lax

KVH = 8
GQ = 4
DH = 128
SLOTS = 1024
Q_DEV = 256
CAP = 128
TABLES = 4
ROWS = 2048


def draw_queries(key, part):
    base = jnp.clip(jax.random.normal(key, (ROWS, KVH, GQ * DH), jnp.float32), -6.0, 6.0)
    return base.astype(jnp.bfloat16)


def draw_cache_keys(key, part):
    base = jnp.clip(jax.random.normal(key, (TABLES, KVH, SLOTS, DH), jnp.float32), -6.0, 6.0)
    return base


def steps_of(rng, extent, split, smallest, top_value):
    gain, own = 1.0, jax.random.fold_in(rng, 6)
    for position, blocks in split:
        steps = jnp.exp(jax.random.uniform(jax.random.fold_in(own, position), (blocks,), jnp.float32, smallest / len(split), top_value / len(split)))
        gain = gain * jnp.repeat(steps, extent[position] // blocks).reshape([-1 if axis == position else 1 for axis in range(len(extent))])
    return gain


def shared_out(rng, own, number, rows, number_of, top, reach, skew):
    ranking = jax.random.permutation(rng, number_of)
    heavy_load, usual = portions_of(number_of, rows * top, reach, skew, True), portions_of(number_of, rows * top, reach, skew, False)
    places = jnp.arange(number_of)

    def named(lengths, turn):
        used = int((lengths > 0).sum())
        fixed = max(1, used // 4)
        shifted = fixed + (places - fixed + turn * (used - fixed)) % max(1, number_of - fixed)
        return jnp.zeros((number_of,), jnp.int32).at[ranking[jnp.where(places < fixed, places, shifted)]].set(jnp.asarray(lengths, jnp.int32))

    lengths = jnp.where(number % 4 == 0, named(heavy_load, number // 4), named(usual, number - number // 4 - 1))
    mixed = jax.random.permutation(jax.random.fold_in(own, 3), number_of)
    donor, taker = mixed[0:number_of // 2 * 2:2], mixed[1:number_of // 2 * 2:2]
    margin = jnp.minimum(lengths[donor] - 1, reach - lengths[taker]) // 2
    margin = jnp.where((donor == ranking[0]) | (taker == ranking[0]) | (lengths[taker] == 0), 0, jnp.maximum(margin, 0))
    shifted = jax.random.randint(jax.random.fold_in(own, 4), (number_of // 2,), 0, 1 << 20) % (margin + 1)
    lengths = lengths.at[donor].add(-shifted).at[taker].add(shifted)
    members = jnp.searchsorted(jnp.cumsum(lengths), jnp.arange(rows * top), side="right").astype(jnp.int32)
    table = members.reshape(top, rows).T
    table = table[jax.random.permutation(jax.random.fold_in(own, 1), rows)]
    turn = jax.random.randint(jax.random.fold_in(own, 2), (rows, 1), 0, top)
    return jnp.take_along_axis(table, (jnp.arange(top)[None, :] + turn) % top, axis=1)


def portions_of(amount, total, reach, slope, full):
    weights = [(1 << 20) // math.isqrt(grade ** slope) + 1 for grade in range(1, amount + 1)]
    largest = reach if full else min(reach, max(-(-total // amount), total * weights[0] // sum(weights)))
    least = 1 if total - largest >= amount - 1 else 0
    given, surplus = [largest] + [least] * (amount - 1), total - largest - least * (amount - 1)
    while surplus > 0:
        candidates = [i for i in range(1, amount) if given[i] < largest] or [i for i in range(1, amount) if given[i] < reach]
        mass, left = sum([weights[i] for i in candidates]), surplus
        for i in candidates:
            extra = min(reach - given[i], max(1, left * weights[i] // mass), surplus)
            given[i] = given[i] + extra
            surplus = surplus - extra
    return np.array(given)


def centred(rng, dims, spread, most, split=(), kind=jnp.bfloat16):
    result = jax.random.normal(rng, dims, jnp.float32) * spread
    if len(split) > 0:
        result = steps_of(rng, dims, split, -0.22, 0.18) * result
    return jnp.clip(result, min=-most, max=most).astype(kind)


def setup_inputs(seed: int = 0, part: int = 0) -> dict:
    seeds = jax.random.split(jax.random.key(seed), 10)
    part_splits = jax.random.split(jax.random.fold_in(seeds[9], part), 10)
    queries = draw_queries(jax.random.fold_in(jax.random.fold_in(seeds[9], part), 71), part)
    cotangent = centred(part_splits[1], (ROWS, KVH, GQ * DH), 1.0, 6.0, ((0, 8), (1, 2)))
    own_kv = centred(part_splits[2], (ROWS, KVH, 2 * DH), 1.0, 6.0, ((0, 8), (1, 2)))
    tables_keys = jax.random.split(jax.random.fold_in(part_splits[3], 1), ROWS // Q_DEV)
    tables_turns = jax.random.permutation(jax.random.fold_in(part_splits[3], 3), ROWS // Q_DEV)
    tables = jax.vmap(lambda own, number: shared_out(jax.random.fold_in(part_splits[3], 2), own, number, Q_DEV, TABLES, 1, CAP, 2))(tables_keys, tables_turns).reshape((ROWS, 1))
    table_owner = jax.random.permutation(part_splits[4], TABLES).astype(jnp.int32)
    cache_keys = draw_cache_keys(jax.random.fold_in(jax.random.fold_in(seeds[9], part), 71), part)
    cache_values = centred(part_splits[6], (TABLES, KVH, SLOTS, DH), 1.0, 6.0, ((0, 4), (1, 2), (2, 2)), jnp.float32)
    first_moment = centred(part_splits[7], (2, TABLES, KVH, SLOTS, DH), 0.05, 0.75, ((1, 4), (2, 2), (3, 2)), jnp.float32)
    second_moment = jnp.clip(jnp.exp(math.log(0.1) - 11.512925 * jax.random.uniform(part_splits[8], (2, TABLES, KVH, SLOTS, DH), jnp.float32) ** steps_of(part_splits[8], (2, TABLES, KVH, SLOTS, DH), ((1, 4), (2, 2), (3, 2)), -0.2, 0.2)), 9.999999974752427e-07, 0.1)
    return dict(queries=queries, cotangent=cotangent, own_kv=own_kv, tables=tables, table_owner=table_owner, cache_keys=cache_keys, cache_values=cache_values, first_moment=first_moment, second_moment=second_moment)


def rounded(x):
    return lax.optimization_barrier(x.astype(jnp.bfloat16)).astype(jnp.float32)

def one_owner(args):
    q_rows, c_rows, kv_rows, keys_bf, vals_bf = args
    count = q_rows.shape[0]
    scale = DH ** (-0.5)
    qf = q_rows.astype(jnp.float32).reshape(count, KVH, GQ, DH)
    cf = c_rows.astype(jnp.float32).reshape(count, KVH, GQ, DH)
    kself = kv_rows[:, :, :DH].astype(jnp.float32)
    vself = kv_rows[:, :, DH:].astype(jnp.float32)
    kf = keys_bf.astype(jnp.float32)
    vf = vals_bf.astype(jnp.float32)
    score = jnp.einsum('nkgd,ksd->nkgs', qf, kf) * scale
    own = jnp.einsum('nkgd,nkd->nkg', qf, kself) * scale
    top = jnp.maximum(lax.optimization_barrier(jnp.max(score, axis=-1)), own)
    expo = jnp.exp(score - top[..., None])
    self_exp = jnp.exp(own - top)
    total = lax.optimization_barrier(jnp.sum(expo, axis=-1)) + self_exp
    prob = expo / total[..., None]
    self_prob = self_exp / total
    weights = rounded(prob)
    self_weight = rounded(self_prob)
    out = jnp.einsum('nkgs,ksd->nkgd', weights, vf) + self_weight[..., None] * vself[:, :, None, :]
    delta = lax.optimization_barrier(jnp.sum(cf * out, axis=-1))
    dprob = jnp.einsum('nkgd,ksd->nkgs', cf, vf)
    dweights = rounded(prob * (dprob - delta[..., None]))
    grad_keys = jnp.einsum('nkgs,nkgd->ksd', dweights, qf) * scale
    grad_values = jnp.einsum('nkgs,nkgd->ksd', weights, cf)
    return (out.astype(jnp.bfloat16).reshape(count, KVH, GQ * DH), grad_keys, grad_values)

def reference(queries, cotangent, own_kv, tables, table_owner, cache_keys, cache_values, first_moment, second_moment):
    blocks = ROWS // Q_DEV
    dest = table_owner[tables[:, 0]].astype(jnp.int32)
    hit = (dest[:, None] == jnp.arange(TABLES, dtype=jnp.int32)[None, :]).astype(jnp.int32)
    hit = hit.reshape(blocks, Q_DEV, TABLES)
    before = jnp.cumsum(hit, axis=1, dtype=jnp.int32) - hit
    rank = lax.optimization_barrier(jnp.sum(before * hit, axis=2, dtype=jnp.int32))
    block_ids = jnp.arange(blocks, dtype=jnp.int32)[:, None]
    place = (dest.reshape(blocks, Q_DEV) * (blocks * CAP) + block_ids * CAP + rank).reshape(-1)

    def pack(x):
        empty = jnp.zeros((TABLES * blocks * CAP,) + x.shape[1:], x.dtype)
        return empty.at[place].set(x).reshape((TABLES, blocks * CAP) + x.shape[1:])
    keys_bf = cache_keys.astype(jnp.bfloat16)
    vals_bf = cache_values.astype(jnp.bfloat16)
    answers, grad_keys, grad_values = lax.map(one_owner, (pack(queries), pack(cotangent), pack(own_kv), keys_bf, vals_bf))
    attended = answers.reshape((TABLES * blocks * CAP,) + answers.shape[2:])[place]
    grad = jnp.stack([grad_keys, grad_values])
    new_first = 0.9 * first_moment + 0.1 * grad
    new_second = 0.95 * second_moment + 0.05 * grad * grad
    params = jnp.stack([cache_keys, cache_values])
    updated = params - 0.02 * new_first / (jnp.sqrt(new_second) + 1e-08)
    return (attended, updated[0], updated[1], new_first, new_second)
```

```python
import functools

import jax
import jax.numpy as jnp
from jax import lax
from jax.experimental import pallas as pl
from jax.experimental.pallas import tpu as pltpu
from jax.sharding import PartitionSpec as P

MESH = pl.DeviceIdType.MESH


def dot(a, b, ca, cb):
    return lax.dot_general(a, b, (((ca,), (cb,)), ((), ())), preferred_element_type=jnp.float32)


def kernel(
    n,
    cap,
    owner_of,
    tables,
    queries,
    cotangent,
    own_kv,
    keys,
    values,
    attended,
    grad,
    cache,
    stash,
    local,
    half_out,
    half_in,
    chain_in,
    pf_send,
    pf_recv,
    zf_send,
    zf_recv,
    pb_send,
    pb_recv,
    zb_send,
    zb_recv,
):
    z = lax.axis_index("owner")
    r = lax.axis_index("rep")
    heads, tokens, width = queries.shape
    dh = keys.shape[2]
    slots = keys.shape[1]
    groups = width // dh
    scale = dh ** (-0.5)
    is_end = jnp.logical_or(z == 0, z == n - 1)
    bf16 = jnp.bfloat16
    f32 = jnp.float32

    def to_partner(src, dst, s_sem, r_sem):
        return pltpu.make_async_remote_copy(
            src_ref=src, dst_ref=dst, send_sem=s_sem, recv_sem=r_sem,
            device_id={"rep": 1 - r}, device_id_type=MESH,
        )

    def to_owner(src, dst, s_sem, r_sem, where):
        return pltpu.make_async_remote_copy(
            src_ref=src, dst_ref=dst, send_sem=s_sem, recv_sem=r_sem,
            device_id={"owner": where}, device_id_type=MESH,
        )

    def share_half(t, h):
        return to_partner(cache.at[t, h, r], cache.at[t, h, r], pf_send.at[t, h], pf_recv.at[t, h])

    def pass_on(t, h, step):
        return to_owner(
            cache.at[t, h, r], cache.at[t, h, r],
            zf_send.at[(step + 1) // 2, t, h], zf_recv.at[t, h], z + step,
        )

    def share_grad(t, h):
        return to_partner(half_out.at[t, h], half_in.at[t, h], pb_send.at[t, h], pb_recv.at[t, h])

    def chain(t, h, step):
        slot = t if step == 1 else jnp.where(t == z + step, n, t)
        return to_owner(
            half_in.at[t, h], chain_in.at[slot, h], zb_send.at[t, h], zb_recv.at[slot, h], z + step
        )

    barrier = pltpu.get_barrier_semaphore()
    pl.semaphore_signal(barrier, inc=1, device_id={"rep": 1 - r}, device_id_type=MESH)

    @pl.when(z > 0)
    def _():
        pl.semaphore_signal(barrier, inc=1, device_id={"owner": z - 1}, device_id_type=MESH)

    @pl.when(z < n - 1)
    def _():
        pl.semaphore_signal(barrier, inc=1, device_id={"owner": z + 1}, device_id_type=MESH)

    def cast(h, carry):
        cache[z, h, r, 0] = keys[h].astype(bf16)
        cache[z, h, r, 1] = values[h].astype(bf16)
        return carry

    lax.fori_loop(0, heads, cast, 0)
    peers = 1 + jnp.where(z > 0, 1, 0) + jnp.where(z < n - 1, 1, 0)
    pl.semaphore_wait(barrier, peers)

    def first(h, carry):
        @pl.when(z > 0)
        def _():
            pass_on(z, h, -1).start()

        @pl.when(z < n - 1)
        def _():
            pass_on(z, h, 1).start()

        share_half(z, h).start()
        return carry

    lax.fori_loop(0, heads, first, 0)

    dest = jnp.zeros((1, tokens), jnp.int32)
    for i in range(owner_of.shape[0]):
        dest = jnp.where(tables[...] == i, owner_of[i], dest)
    earlier = (
        lax.broadcasted_iota(jnp.int32, (tokens, tokens), 0)
        < lax.broadcasted_iota(jnp.int32, (tokens, tokens), 1)
    ).astype(f32).astype(bf16)
    attended[...] = jnp.zeros(attended.shape, attended.dtype)

    def receive(pair, side):
        d = 1 + pair // heads
        h = lax.rem(pair, heads)
        t = z - d if side == 0 else z + d
        there = t >= 0 if side == 0 else t < n

        @pl.when(jnp.logical_and(jnp.logical_and(pair >= 0, pair < (n - 1) * heads), there))
        def _():
            pass_on(t, h, 1 if side == 0 else -1).wait_recv()

            if side == 0:
                @pl.when(z < n - 1)
                def _():
                    pass_on(t, h, 1).start()
            else:
                @pl.when(z > 0)
                def _():
                    pass_on(t, h, -1).start()

            share_half(t, h).start()

    def compute(t, h):
        share_half(t, h).wait_recv()
        hit = dest == t
        hits = jnp.broadcast_to(hit.astype(f32), (8, tokens)).astype(bf16)
        rank = dot(hits, earlier, 1, 0)[:1].astype(jnp.int32)
        pick = jnp.logical_and(
            lax.broadcasted_iota(jnp.int32, (cap, tokens), 0) == rank, hit
        ).astype(f32).astype(bf16)

        def rows(x):
            return jnp.concatenate([x[:, g * dh:(g + 1) * dh] for g in range(groups)], axis=0)

        q = rows(dot(pick, queries[h], 1, 0))
        c = rows(dot(pick, cotangent[h], 1, 0))
        kv = dot(pick, own_kv[h], 1, 0)
        kself = jnp.concatenate([kv[:, :dh]] * groups, axis=0)
        vself = jnp.concatenate([kv[:, dh:]] * groups, axis=0)
        own = jnp.sum(jnp.transpose(q * kself), axis=0, keepdims=True) * scale
        qb = q.astype(bf16)
        cb = c.astype(bf16)
        k = cache[t, h, :, 0].reshape(2 * slots, dh)
        v = cache[t, h, :, 1].reshape(2 * slots, dh)
        score = dot(k, qb, 1, 1) * scale
        top = jnp.maximum(jnp.max(score, axis=0, keepdims=True), own)
        expo = jnp.exp(score - top)
        self_exp = jnp.exp(own - top)
        total = jnp.sum(expo, axis=0, keepdims=True) + self_exp
        inv = 1.0 / total
        prob = expo * inv
        self_weight = (self_exp * inv).astype(bf16).astype(f32)
        weights = prob.astype(bf16)
        out = dot(v, weights, 0, 0) + self_weight * jnp.transpose(vself)
        delta = jnp.sum(jnp.transpose(c) * out, axis=0, keepdims=True)
        dprob = dot(v, cb, 1, 1)
        dweights = (prob * (dprob - delta)).astype(bf16)
        gk = dot(dweights, qb, 1, 0) * scale
        gv = dot(weights, cb, 1, 0)
        for i in range(2):
            local[i, 0] = gk[i * slots:(i + 1) * slots]
            local[i, 1] = gv[i * slots:(i + 1) * slots]
        half_out[t, h] = local[1 - r].astype(bf16)
        share_grad(t, h).start()
        stash[t, h] = local[r]
        answer = jnp.transpose(out).astype(bf16)
        answer = jnp.concatenate([answer[g * cap:(g + 1) * cap] for g in range(groups)], axis=1)
        attended[h] = (attended[h].astype(f32) + dot(pick, answer, 0, 0)).astype(bf16)

    def finish(pair, right):
        level = 1 + pair // heads
        h = lax.rem(pair, heads)
        t = level if right else n - 1 - level
        there = t > z if right else t < z
        step = 1 if right else -1

        @pl.when(jnp.logical_and(jnp.logical_and(pair >= 0, pair < (n - 1) * heads), there))
        def _():
            share_grad(t, h).wait_recv()

            @pl.when(z > 0 if right else z < n - 1)
            def _():
                to_owner(
                    half_in.at[t, h], chain_in.at[t, h], zb_send.at[t, h], zb_recv.at[t, h],
                    z - step,
                ).wait_recv()
                stash[t, h] = stash[t, h] + chain_in[t, h].astype(f32)

            half_in[t, h] = (stash[t, h] + half_in[t, h].astype(f32)).astype(bf16)
            chain(t, h, step).start()

    def body(m, carry):
        pair = m - jnp.where(is_end, heads - 1, 0)
        receive(pair, 0)
        receive(pair, 1)

        def one(side, carry):
            d = m // heads
            h = lax.rem(m, heads)
            t = z - d + 2 * d * side
            there = jnp.logical_and(jnp.logical_and(t >= 0, t < n), jnp.logical_or(d > 0, side == 0))

            @pl.when(jnp.logical_and(there, m < n * heads))
            def _():
                compute(t, h)

            return carry

        lax.fori_loop(0, 2, one, 0)
        done = m - heads - jnp.where(is_end, 1, 0)

        @pl.when(2 * z < n - 1)
        def _():
            finish(done, True)
            finish(done, False)

        @pl.when(2 * z >= n - 1)
        def _():
            finish(done, False)
            finish(done, True)

        return carry

    lax.fori_loop(0, n * heads + 1, body, 0)

    def last(h, carry):
        share_grad(z, h).wait_recv()
        total = stash[z, h] + half_in[z, h].astype(f32)
        stash[z, h] = total

        @pl.when(z > 0)
        def _():
            to_owner(
                half_in.at[z, h], chain_in.at[z, h], zb_send.at[z, h], zb_recv.at[z, h], z - 1
            ).wait_recv()
            stash[z, h] = stash[z, h] + chain_in[z, h].astype(f32)

        @pl.when(z < n - 1)
        def _():
            to_owner(
                half_in.at[z, h], chain_in.at[n, h], zb_send.at[z, h], zb_recv.at[n, h], z + 1
            ).wait_recv()
            stash[z, h] = stash[z, h] + chain_in[n, h].astype(f32)

        grad[0, h] = stash[z, h, 0]
        grad[1, h] = stash[z, h, 1]
        return carry

    lax.fori_loop(0, heads, last, 0)

    def drain(i, carry):
        t = i // heads
        h = lax.rem(i, heads)
        share_half(t, h).wait_send()
        share_grad(t, h).wait_send()

        @pl.when(jnp.logical_and(t <= z, z < n - 1))
        def _():
            pass_on(t, h, 1).wait_send()

        @pl.when(jnp.logical_and(t >= z, z > 0))
        def _():
            pass_on(t, h, -1).wait_send()

        @pl.when(t > z)
        def _():
            chain(t, h, 1).wait_send()

        @pl.when(t < z)
        def _():
            chain(t, h, -1).wait_send()

        return carry

    lax.fori_loop(0, n * heads, drain, 0)


def attend(n, owner_of, tables, queries, cotangent, own_kv, keys, values):
    heads, tokens, width = queries.shape
    slots, dh = keys.shape[1:]
    cap = 2 * tokens // n
    vmem = pl.BlockSpec(memory_space=pltpu.VMEM)
    dma = pltpu.SemaphoreType.DMA
    bf16 = jnp.bfloat16
    piece = (heads, 2, slots, dh)
    return pl.pallas_call(
        functools.partial(kernel, n, cap),
        out_shape=(
            jax.ShapeDtypeStruct((heads, tokens, width), bf16),
            jax.ShapeDtypeStruct((2, heads, slots, dh), jnp.float32),
        ),
        in_specs=[pl.BlockSpec(memory_space=pltpu.SMEM)] + [vmem] * 6,
        out_specs=(vmem, vmem),
        scratch_shapes=[
            pltpu.VMEM((n, heads, 2, 2, slots, dh), bf16),
            pltpu.VMEM((n,) + piece, jnp.float32),
            pltpu.VMEM((2, 2, slots, dh), jnp.float32),
            pltpu.VMEM((n,) + piece, bf16),
            pltpu.VMEM((n,) + piece, bf16),
            pltpu.VMEM((n + 1,) + piece, bf16),
            dma((n, heads)),
            dma((n, heads)),
            dma((2, n, heads)),
            dma((n, heads)),
            dma((n, heads)),
            dma((n, heads)),
            dma((n, heads)),
            dma((n + 1, heads)),
        ],
        compiler_params=pltpu.CompilerParams(
            collective_id=0, has_side_effects=True, vmem_limit_bytes=62 * 1024 * 1024
        ),
    )(owner_of, tables, queries, cotangent, own_kv, keys, values)


def per_device(
    queries,
    cotangent,
    own_kv,
    tables,
    table_owner,
    cache_keys,
    cache_values,
    first_moment,
    second_moment,
):
    n = lax.axis_size("owner")
    attended, grad = attend(
        n,
        table_owner,
        tables.reshape(1, -1),
        jnp.swapaxes(queries, 0, 1),
        jnp.swapaxes(cotangent, 0, 1),
        jnp.swapaxes(own_kv, 0, 1),
        cache_keys[0],
        cache_values[0],
    )
    attended = jnp.swapaxes(attended, 0, 1)
    grad = grad[:, None]
    new_first = 0.9 * first_moment + 0.1 * grad
    new_second = 0.95 * second_moment + 0.05 * grad * grad
    step = 0.02 * new_first / (jnp.sqrt(new_second) + 1e-08)
    return (attended, cache_keys - step[0], cache_values - step[1], new_first, new_second)


def solution(mesh):
    in_specs = (
        P(("groups", "owner", "rep"), "head", None),
        P(("groups", "owner", "rep"), "head", None),
        P(("groups", "owner", "rep"), "head", None),
        P(("groups", "owner", "rep"), None),
        P("groups"),
        P(("groups", "owner"), "head", "rep", None),
        P(("groups", "owner"), "head", "rep", None),
        P(None, ("groups", "owner"), "head", "rep", None),
        P(None, ("groups", "owner"), "head", "rep", None),
    )
    out_specs = (
        P(("groups", "owner", "rep"), "head", None),
        P(("groups", "owner"), "head", "rep", None),
        P(("groups", "owner"), "head", "rep", None),
        P(None, ("groups", "owner"), "head", "rep", None),
        P(None, ("groups", "owner"), "head", "rep", None),
    )
    return jax.shard_map(
        per_device, mesh=mesh, in_specs=in_specs, out_specs=out_specs, check_vma=False
    )
```

```python
import functools

import jax
import jax.numpy as jnp
from jax import lax
from jax.experimental import pallas as pl
from jax.experimental.pallas import tpu as pltpu
from jax.sharding import PartitionSpec as P

MESH = pl.DeviceIdType.MESH


def dot(a, b, ca, cb):
    return lax.dot_general(a, b, (((ca,), (cb,)), ((), ())), preferred_element_type=jnp.float32)


def kernel(
    n,
    cap,
    owner_of,
    tables,
    queries_in,
    cotangent_in,
    own_kv_in,
    keys,
    values,
    attended,
    grad,
    queries,
    cotangent,
    own_kv,
    cache,
    stash,
    local,
    half_out,
    half_in,
    chain_in,
    pf_send,
    pf_recv,
    zf_send,
    zf_recv,
    pb_send,
    pb_recv,
    zb_send,
    zb_recv,
):
    z = lax.axis_index("owner")
    r = lax.axis_index("rep")
    heads, tokens, width = queries.shape
    dh = keys.shape[2]
    slots = keys.shape[1]
    parts = half_in.shape[2]
    part = slots // parts
    groups = width // dh
    scale = dh ** (-0.5)
    is_end = jnp.logical_or(z == 0, z == n - 1)
    bf16 = jnp.bfloat16
    f32 = jnp.float32

    def to_partner(src, dst, s_sem, r_sem):
        return pltpu.make_async_remote_copy(
            src_ref=src, dst_ref=dst, send_sem=s_sem, recv_sem=r_sem,
            device_id={"rep": 1 - r}, device_id_type=MESH,
        )

    def to_owner(src, dst, s_sem, r_sem, where):
        return pltpu.make_async_remote_copy(
            src_ref=src, dst_ref=dst, send_sem=s_sem, recv_sem=r_sem,
            device_id={"owner": where}, device_id_type=MESH,
        )

    def share_half(t, h, u):
        return to_partner(
            cache.at[t, h, r, u], cache.at[t, h, r, u], pf_send.at[t, h, u], pf_recv.at[t, h, u]
        )

    def pass_on(t, h, u, step):
        return to_owner(
            cache.at[t, h, r, u], cache.at[t, h, r, u],
            zf_send.at[(step + 1) // 2, t, h, u], zf_recv.at[t, h, u], z + step,
        )

    def share_grad(t, h, u):
        return to_partner(
            half_out.at[t, h, u], half_in.at[t, h, u], pb_send.at[t, h, u], pb_recv.at[t, h, u]
        )

    def chain_to(t, h, u, slot, where):
        return to_owner(
            half_in.at[t, h, u], chain_in.at[slot, h, u],
            zb_send.at[t, h, u], zb_recv.at[slot, h, u], where,
        )

    def chain(t, h, u, step):
        slot = t if step == 1 else jnp.where(t == z + step, n, t)
        return chain_to(t, h, u, slot, z + step)

    barrier = pltpu.get_barrier_semaphore()
    pl.semaphore_signal(barrier, inc=1, device_id={"rep": 1 - r}, device_id_type=MESH)

    @pl.when(z > 0)
    def _():
        pl.semaphore_signal(barrier, inc=1, device_id={"owner": z - 1}, device_id_type=MESH)

    @pl.when(z < n - 1)
    def _():
        pl.semaphore_signal(barrier, inc=1, device_id={"owner": z + 1}, device_id_type=MESH)

    def cast(h, carry):
        for u in range(parts):
            cache[z, h, r, u, 0] = keys[h, u * part:(u + 1) * part].astype(bf16)
            cache[z, h, r, u, 1] = values[h, u * part:(u + 1) * part].astype(bf16)
        return carry

    lax.fori_loop(0, heads, cast, 0)
    peers = 1 + jnp.where(z > 0, 1, 0) + jnp.where(z < n - 1, 1, 0)
    pl.semaphore_wait(barrier, peers)

    def first(h, carry):
        for u in range(parts):
            @pl.when(z > 0)
            def _():
                pass_on(z, h, u, -1).start()

            @pl.when(z < n - 1)
            def _():
                pass_on(z, h, u, 1).start()

            share_half(z, h, u).start()
        return carry

    lax.fori_loop(0, heads, first, 0)

    for h in range(heads):
        queries[h] = queries_in[:, h, :]
        cotangent[h] = cotangent_in[:, h, :]
        own_kv[h] = own_kv_in[:, h, :]
    dest = jnp.zeros((1, tokens), jnp.int32)
    for i in range(owner_of.shape[0]):
        dest = jnp.where(tables[...] == i, owner_of[i], dest)
    earlier = (
        lax.broadcasted_iota(jnp.int32, (tokens, tokens), 0)
        < lax.broadcasted_iota(jnp.int32, (tokens, tokens), 1)
    ).astype(f32).astype(bf16)
    attended[...] = jnp.zeros(attended.shape, attended.dtype)

    def receive(pair, side):
        d = 1 + pair // heads
        h = lax.rem(pair, heads)
        t = z - d if side == 0 else z + d
        there = t >= 0 if side == 0 else t < n

        @pl.when(jnp.logical_and(jnp.logical_and(pair >= 0, pair < (n - 1) * heads), there))
        def _():
            for u in range(parts):
                pass_on(t, h, u, 1 if side == 0 else -1).wait_recv()

                if side == 0:
                    @pl.when(z < n - 1)
                    def _():
                        pass_on(t, h, u, 1).start()
                else:
                    @pl.when(z > 0)
                    def _():
                        pass_on(t, h, u, -1).start()

                share_half(t, h, u).start()

    def compute(t, h):
        for u in range(parts):
            share_half(t, h, u).wait_recv()
        hit = dest == t
        hits = jnp.broadcast_to(hit.astype(f32), (8, tokens)).astype(bf16)
        rank = dot(hits, earlier, 1, 0)[:1].astype(jnp.int32)
        pick = jnp.logical_and(
            lax.broadcasted_iota(jnp.int32, (cap, tokens), 0) == rank, hit
        ).astype(f32).astype(bf16)

        def rows(x):
            return jnp.concatenate([x[:, g * dh:(g + 1) * dh] for g in range(groups)], axis=0)

        q = rows(dot(pick, queries[h], 1, 0))
        c = rows(dot(pick, cotangent[h], 1, 0))
        kv = dot(pick, own_kv[h], 1, 0)
        kself = jnp.concatenate([kv[:, :dh]] * groups, axis=0)
        vself = jnp.concatenate([kv[:, dh:]] * groups, axis=0)
        own = jnp.sum(jnp.transpose(q * kself), axis=0, keepdims=True) * scale
        qb = q.astype(bf16)
        cb = c.astype(bf16)
        k = cache[t, h, :, :, 0].reshape(2 * slots, dh)
        v = cache[t, h, :, :, 1].reshape(2 * slots, dh)
        score = dot(k, qb, 1, 1) * scale
        top = jnp.maximum(jnp.max(score, axis=0, keepdims=True), own)
        expo = jnp.exp(score - top)
        self_exp = jnp.exp(own - top)
        total = jnp.sum(expo, axis=0, keepdims=True) + self_exp
        inv = 1.0 / total
        prob = expo * inv
        self_weight = (self_exp * inv).astype(bf16).astype(f32)
        weights = prob.astype(bf16)
        out = dot(v, weights, 0, 0) + self_weight * jnp.transpose(vself)
        delta = jnp.sum(jnp.transpose(c) * out, axis=0, keepdims=True)
        dprob = dot(v, cb, 1, 1)
        dweights = (prob * (dprob - delta)).astype(bf16)
        gk = dot(dweights, qb, 1, 0) * scale
        gv = dot(weights, cb, 1, 0)
        for i in range(2):
            for u in range(parts):
                at = i * slots + u * part
                local[i, u, 0] = gk[at:at + part]
                local[i, u, 1] = gv[at:at + part]
        for u in range(parts):
            half_out[t, h, u] = local[1 - r, u].astype(bf16)
            share_grad(t, h, u).start()
        stash[t, h] = local[r]
        answer = jnp.transpose(out).astype(bf16)
        answer = jnp.concatenate([answer[g * cap:(g + 1) * cap] for g in range(groups)], axis=1)
        attended[h] = (attended[h].astype(f32) + dot(pick, answer, 0, 0)).astype(bf16)

    def finish(pair, right):
        level = 1 + pair // heads
        h = lax.rem(pair, heads)
        t = level if right else n - 1 - level
        there = t > z if right else t < z
        step = 1 if right else -1

        @pl.when(jnp.logical_and(jnp.logical_and(pair >= 0, pair < (n - 1) * heads), there))
        def _():
            for u in range(parts):
                share_grad(t, h, u).wait_recv()

                @pl.when(z > 0 if right else z < n - 1)
                def _():
                    chain_to(t, h, u, t, z - step).wait_recv()
                    stash[t, h, u] = stash[t, h, u] + chain_in[t, h, u].astype(f32)

                half_in[t, h, u] = (stash[t, h, u] + half_in[t, h, u].astype(f32)).astype(bf16)
                chain(t, h, u, step).start()

    def body(m, carry):
        pair = m - jnp.where(is_end, heads - 1, 0)
        receive(pair, 0)
        receive(pair, 1)

        def one(side, carry):
            d = m // heads
            h = lax.rem(m, heads)
            t = z - d + 2 * d * side
            there = jnp.logical_and(jnp.logical_and(t >= 0, t < n), jnp.logical_or(d > 0, side == 0))

            @pl.when(jnp.logical_and(there, m < n * heads))
            def _():
                compute(t, h)

            return carry

        lax.fori_loop(0, 2, one, 0)
        done = m - heads - jnp.where(is_end, 1, 0)

        @pl.when(2 * z < n - 1)
        def _():
            finish(done, True)
            finish(done, False)

        @pl.when(2 * z >= n - 1)
        def _():
            finish(done, False)
            finish(done, True)

        return carry

    lax.fori_loop(0, n * heads + 1, body, 0)

    def last(h, carry):
        for u in range(parts):
            share_grad(z, h, u).wait_recv()
            stash[z, h, u] = stash[z, h, u] + half_in[z, h, u].astype(f32)

            @pl.when(z > 0)
            def _():
                chain_to(z, h, u, z, z - 1).wait_recv()
                stash[z, h, u] = stash[z, h, u] + chain_in[z, h, u].astype(f32)

            @pl.when(z < n - 1)
            def _():
                chain_to(z, h, u, n, z + 1).wait_recv()
                stash[z, h, u] = stash[z, h, u] + chain_in[n, h, u].astype(f32)

            grad[0, h, u * part:(u + 1) * part] = stash[z, h, u, 0]
            grad[1, h, u * part:(u + 1) * part] = stash[z, h, u, 1]
        return carry

    lax.fori_loop(0, heads, last, 0)

    def drain(i, carry):
        t = i // heads
        h = lax.rem(i, heads)
        for u in range(parts):
            share_half(t, h, u).wait_send()
            share_grad(t, h, u).wait_send()

            @pl.when(jnp.logical_and(t <= z, z < n - 1))
            def _():
                pass_on(t, h, u, 1).wait_send()

            @pl.when(jnp.logical_and(t >= z, z > 0))
            def _():
                pass_on(t, h, u, -1).wait_send()

            @pl.when(t > z)
            def _():
                chain(t, h, u, 1).wait_send()

            @pl.when(t < z)
            def _():
                chain(t, h, u, -1).wait_send()

        return carry

    lax.fori_loop(0, n * heads, drain, 0)


def attend(n, owner_of, tables, queries, cotangent, own_kv, keys, values):
    tokens, heads, width = queries.shape
    slots, dh = keys.shape[1:]
    cap = 2 * tokens // n
    vmem = pl.BlockSpec(memory_space=pltpu.VMEM)
    dma = pltpu.SemaphoreType.DMA
    bf16 = jnp.bfloat16
    parts = 2
    piece = (heads, parts, 2, slots // parts, dh)
    return pl.pallas_call(
        functools.partial(kernel, n, cap),
        out_shape=(
            jax.ShapeDtypeStruct((heads, tokens, width), bf16),
            jax.ShapeDtypeStruct((2, heads, slots, dh), jnp.float32),
        ),
        in_specs=[pl.BlockSpec(memory_space=pltpu.SMEM)] + [vmem] * 6,
        out_specs=(vmem, vmem),
        scratch_shapes=[
            pltpu.VMEM((heads, tokens, width), bf16),
            pltpu.VMEM((heads, tokens, width), bf16),
            pltpu.VMEM((heads, tokens, 2 * dh), bf16),
            pltpu.VMEM((n, heads, 2, parts, 2, slots // parts, dh), bf16),
            pltpu.VMEM((n,) + piece, jnp.float32),
            pltpu.VMEM((2, parts, 2, slots // parts, dh), jnp.float32),
            pltpu.VMEM((n,) + piece, bf16),
            pltpu.VMEM((n,) + piece, bf16),
            pltpu.VMEM((n + 1,) + piece, bf16),
            dma((n, heads, parts)),
            dma((n, heads, parts)),
            dma((2, n, heads, parts)),
            dma((n, heads, parts)),
            dma((n, heads, parts)),
            dma((n, heads, parts)),
            dma((n, heads, parts)),
            dma((n + 1, heads, parts)),
        ],
        compiler_params=pltpu.CompilerParams(
            collective_id=0, has_side_effects=True, vmem_limit_bytes=62 * 1024 * 1024
        ),
    )(owner_of, tables, queries, cotangent, own_kv, keys, values)


def per_device(
    queries,
    cotangent,
    own_kv,
    tables,
    table_owner,
    cache_keys,
    cache_values,
    first_moment,
    second_moment,
):
    n = lax.axis_size("owner")
    attended, grad = attend(
        n,
        table_owner,
        tables.reshape(1, -1),
        queries,
        cotangent,
        own_kv,
        cache_keys[0],
        cache_values[0],
    )
    attended = jnp.swapaxes(attended, 0, 1)
    grad = grad[:, None]
    new_first = 0.9 * first_moment + 0.1 * grad
    new_second = 0.95 * second_moment + 0.05 * grad * grad
    step = 0.02 * new_first / (jnp.sqrt(new_second) + 1e-08)
    return (attended, cache_keys - step[0], cache_values - step[1], new_first, new_second)


def solution(mesh):
    in_specs = (
        P(("groups", "owner", "rep"), "head", None),
        P(("groups", "owner", "rep"), "head", None),
        P(("groups", "owner", "rep"), "head", None),
        P(("groups", "owner", "rep"), None),
        P("groups"),
        P(("groups", "owner"), "head", "rep", None),
        P(("groups", "owner"), "head", "rep", None),
        P(None, ("groups", "owner"), "head", "rep", None),
        P(None, ("groups", "owner"), "head", "rep", None),
    )
    out_specs = (
        P(("groups", "owner", "rep"), "head", None),
        P(("groups", "owner"), "head", "rep", None),
        P(("groups", "owner"), "head", "rep", None),
        P(None, ("groups", "owner"), "head", "rep", None),
        P(None, ("groups", "owner"), "head", "rep", None),
    )
    return jax.shard_map(
        per_device, mesh=mesh, in_specs=in_specs, out_specs=out_specs, check_vma=False
    )
```
